32 devices in a mesh: groups: 2 (over x), seq: 16 (over z, y, core).
Axes of the slice: x: 2, y: 2, z: 4, core: 2. Of those that a mesh axis runs over, the one named last changes fastest.
Arguments:
- q_fresh: bfloat16 [5120, 4096], P(('groups', 'seq')), parts along dimension 0, may hold values from -9 to 9, as said below
- k_fresh: bfloat16 [5120, 4096], P(('groups', 'seq')), parts along dimension 0, may hold values from -5.6 to 5.6, as said below
- v_fresh: bfloat16 [5120, 4096], P(('groups', 'seq')), parts along dimension 0, may hold values from -6 to 6
- k_stale: bfloat16 [5120, 4096], P('groups', 'seq'), parts along dimension 0, may hold values from -5.59375 to 5.59375
- v_stale: bfloat16 [5120, 4096], P('groups', 'seq'), parts along dimension 0, may hold values from -6 to 6
- rank: int32 [10], P('groups'), parts along dimension 0, may hold values from 0 to 4, each once
- ends: int32 [10], P('groups'), parts along dimension 0, may hold values from 512 to 2560, as said below
Outputs:
- attended: bfloat16 [5120, 4096], P(('groups', 'seq')), parts along dimension 0
The draws below stay inside these ranges and needn't reach their ends.
There are 2 independent parts, one for each index of `groups`. The reference program is written for one: setup_inputs(seed, part) draws one part's arguments, and reference() takes and returns one part's arrays. A program takes and returns all parts, laid end to end along the dimension named above; each array names one. Nothing has to cross between parts.
Inputs may be any that keep to these rules, and one draw needn't show every extreme that they name: `q_fresh`: queries of both draws lie within this range. `k_fresh`: keys of both draws lie within this range. Multiples of 512, never falling along the patches, ends[p] >= (p + 1) * 512; the first equals 512, the last equals 2560.
All inputs are finite; a program needn't handle non-finite values.
Results may differ from the reference program's by a relative error of at most 0.0036.
Values may be sent and summed in bfloat16 or wider, within the bound.
No kernel may reach another device: no remote copies, remote signals or barrier semaphores. Data moves between devices by JAX's collectives and lax.ppermute only.
A program may use at most 64 MiB of HBM per device.

```python
import math
import jax
import jax.numpy as jnp
from jax import lax

HEADS = 32
HEAD_DIM = 128
PATCH = 512
SPAN = 2560
PATCHES = 5


def query_key_pair(key):
    width = HEADS * HEAD_DIM
    key_query, key_key = jax.random.split(jax.random.fold_in(key, 11), 2)
    query = jnp.clip(1.4 * jax.random.normal(key_query, (SPAN, width), jnp.float32), -5.6, 5.6)
    keys = jnp.clip(1.4 * jax.random.normal(key_key, (SPAN, width), jnp.float32), -5.6, 5.6)
    return (query.astype(jnp.bfloat16), keys.astype(jnp.bfloat16))


def draw_q_fresh(key, part):
    return query_key_pair(key)[0]


def draw_k_fresh(key, part):
    return query_key_pair(key)[1]


def draw_ends(key, part):
    numbers = jnp.arange(PATCHES, dtype=jnp.int32)
    extra = jax.random.randint(jax.random.fold_in(key, 5), (PATCHES,), 0, 4, dtype=jnp.int32)
    extra = jnp.where(numbers > 0, extra, 0)
    raw = (numbers + 1 + extra) * PATCH
    return lax.cummax(jnp.minimum(raw, SPAN), axis=0)


def steps_of(stream_key, shape, shards, least, high):
    factor_of = 1.0
    for position, shards_of in shards:
        heights = jax.random.uniform(jax.random.fold_in(jax.random.fold_in(stream_key, 6), position), (shards_of,), jnp.float32, least / len(shards), high / len(shards))
        factor_of = factor_of * jnp.repeat(jnp.exp(heights), shape[position] // shards_of).reshape((-1,) + (1,) * (len(shape) - 1 - position))
    return factor_of


def scatter_about(rng, extent, scale, most, cuts=(), held_as=jnp.bfloat16):
    drawn = scale * jax.random.normal(rng, extent, jnp.float32)
    if cuts:
        drawn = drawn * steps_of(rng, extent, cuts, -0.22, 0.18)
    return jnp.clip(drawn, -most, most).astype(held_as)


def setup_inputs(seed: int = 0, part: int = 0) -> dict:
    streams_of = jax.random.split(jax.random.key(seed), 8)
    own_keys = jax.random.split(jax.random.fold_in(streams_of[7], part), 8)
    q_fresh = draw_q_fresh(jax.random.fold_in(jax.random.fold_in(streams_of[7], part), 71), part)
    k_fresh = draw_k_fresh(jax.random.fold_in(jax.random.fold_in(streams_of[7], part), 71), part)
    v_fresh = scatter_about(own_keys[2], (SPAN, HEADS * HEAD_DIM), 1.0, 6.0, ((0, 16),))
    k_stale = scatter_about(own_keys[3], (SPAN, HEADS * HEAD_DIM), 1.4, 5.59375, ((1, 16),))
    v_stale = scatter_about(own_keys[4], (SPAN, HEADS * HEAD_DIM), 1.0, 6.0, ((1, 16),))
    rank = jax.random.permutation(own_keys[5], PATCHES).astype(jnp.int32)
    ends = draw_ends(jax.random.fold_in(jax.random.fold_in(streams_of[7], part), 71), part)
    return {"q_fresh": q_fresh, "k_fresh": k_fresh, "v_fresh": v_fresh, "k_stale": k_stale, "v_stale": v_stale, "rank": rank, "ends": ends}


def reference(q_fresh, k_fresh, v_fresh, k_stale, v_stale, rank, ends):
    positions = jnp.arange(SPAN, dtype=jnp.int32)
    key_rank = rank[positions // PATCH]
    scale = 1.0 / math.sqrt(HEAD_DIM)

    def to_heads(a):
        return a.reshape(SPAN, HEADS, HEAD_DIM).transpose(1, 0, 2)
    keys_new, values_new = (to_heads(k_fresh), to_heads(v_fresh))
    keys_old, values_old = (to_heads(k_stale), to_heads(v_stale))

    def one_patch(index):
        start = (index * PATCH).astype(jnp.int32)
        block = lax.dynamic_slice_in_dim(q_fresh, start, PATCH, 0)
        block = block.reshape(PATCH, HEADS, HEAD_DIM).transpose(1, 0, 2)
        fresh = key_rank <= rank[index]
        visible = positions < ends[index]
        keys = jnp.where(fresh[None, :, None], keys_new, keys_old)
        values = jnp.where(fresh[None, :, None], values_new, values_old)

        def one_head(items):
            query, key, value = items
            score = jnp.dot(query, key.T, preferred_element_type=jnp.float32) * scale
            score = jnp.where(visible[None, :], score, -jnp.inf)
            top = lax.optimization_barrier(jnp.max(score, axis=1, keepdims=True))
            weight = jnp.exp(score - top)
            total = lax.optimization_barrier(jnp.sum(weight, axis=1, keepdims=True))
            mixed = jnp.dot(weight.astype(jnp.bfloat16), value, preferred_element_type=jnp.float32)
            return (mixed / total).astype(jnp.bfloat16)
        result = lax.map(one_head, (block, keys, values))
        return result.transpose(1, 0, 2).reshape(PATCH, HEADS * HEAD_DIM)
    pieces = lax.map(one_patch, jnp.arange(PATCHES, dtype=jnp.int32))
    return pieces.reshape(SPAN, HEADS * HEAD_DIM)
```

```python
import functools
import math

import jax
import jax.numpy as jnp
from jax import lax
from jax.experimental import pallas as pl
from jax.experimental.pallas import tpu as pltpu
from jax.sharding import PartitionSpec as P

HEAD_DIM = 128
PATCH = 512


def attend_kernel(rank_ref, ends_ref, q_ref, kf_ref, vf_ref, ks_ref, vs_ref, out_ref, *, scale):
    p = pl.program_id(0)
    mine = rank_ref[p]
    count = ends_ref[p] // PATCH
    rows = q_ref.shape[0] * q_ref.shape[1]
    flat = (rows, HEAD_DIM)
    query = q_ref.reshape(*flat)[pl.ds(pl.multiple_of(p * PATCH, PATCH), PATCH), :]
    keys_new = kf_ref.reshape(*flat)
    values_new = vf_ref.reshape(*flat)

    def step(j, carry):
        top, total, mixed = carry
        at = pl.ds(pl.multiple_of(j * PATCH, PATCH), PATCH)
        fresh = rank_ref[j] <= mine
        keys = jnp.where(fresh, keys_new[at, :], ks_ref[at, :])
        values = jnp.where(fresh, values_new[at, :], vs_ref[at, :])
        score = lax.dot_general(query, keys, (((1,), (1,)), ((), ())), preferred_element_type=jnp.float32) * scale
        higher = jnp.maximum(top, jnp.max(score, axis=1, keepdims=True))
        weight = jnp.exp(score - higher)
        shrink = jnp.exp(top - higher)
        total = total * shrink + jnp.sum(weight, axis=1, keepdims=True)
        mixed = mixed * shrink + jnp.dot(weight.astype(jnp.bfloat16), values, preferred_element_type=jnp.float32)
        return higher, total, mixed

    start = (
        jnp.full((PATCH, 1), -jnp.inf, jnp.float32),
        jnp.zeros((PATCH, 1), jnp.float32),
        jnp.zeros((PATCH, HEAD_DIM), jnp.float32),
    )
    _, total, mixed = lax.fori_loop(0, count, step, start)
    out_ref[...] = (mixed / total).astype(jnp.bfloat16)


def attend(packed, k_stale, v_stale, rank, ends, head):
    shards_here, _, rows_here, _ = packed.shape
    total_rows = shards_here * rows_here
    part = [
        pl.BlockSpec((shards_here, None, rows_here, HEAD_DIM), lambda p, r, e, i=i: (0, i, 0, 0))
        for i in range(3)
    ]
    stale = pl.BlockSpec((total_rows, HEAD_DIM), lambda p, r, e: (0, head))
    return pl.pallas_call(
        functools.partial(attend_kernel, scale=1.0 / math.sqrt(HEAD_DIM)),
        grid_spec=pltpu.PrefetchScalarGridSpec(
            num_scalar_prefetch=2,
            grid=(rank.shape[0],),
            in_specs=[*part, stale, stale],
            out_specs=pl.BlockSpec((PATCH, HEAD_DIM), lambda p, r, e: (p, 0)),
        ),
        out_shape=jax.ShapeDtypeStruct((total_rows, HEAD_DIM), jnp.bfloat16),
        name="attend",
    )(rank, ends, packed, packed, packed, k_stale, v_stale)


def pack_kernel(q_ref, k_ref, v_ref, out_ref, *, head, heads_here):
    for t in range(out_ref.shape[0]):
        at = (t * heads_here + head) * HEAD_DIM
        for i, ref in enumerate((q_ref, k_ref, v_ref)):
            out_ref[t, i] = ref[:, at:at + HEAD_DIM]


def pack(arrays, others, heads_here, head):
    rows_here = arrays[0].shape[0]
    each = math.gcd(others, 4)
    wide = each * heads_here * HEAD_DIM
    return pl.pallas_call(
        functools.partial(pack_kernel, head=head, heads_here=heads_here),
        grid=(others // each,),
        in_specs=[pl.BlockSpec((rows_here, wide), lambda g: (0, g))] * 3,
        out_specs=pl.BlockSpec((each, 3, rows_here, HEAD_DIM), lambda g: (g, 0, 0, 0)),
        out_shape=jax.ShapeDtypeStruct((others, 3, rows_here, HEAD_DIM), jnp.bfloat16),
        name="pack",
    )(*arrays)


def unpack_kernel(*refs):
    out_ref = refs[-1]
    heads_here = len(refs) - 1
    for head in range(heads_here):
        for t in range(refs[head].shape[0]):
            at = (t * heads_here + head) * HEAD_DIM
            out_ref[:, at:at + HEAD_DIM] = refs[head][t]


def unpack(returned):
    heads_here = len(returned)
    others, rows_here, _ = returned[0].shape
    each = math.gcd(others, 4)
    return pl.pallas_call(
        unpack_kernel,
        grid=(others // each,),
        in_specs=[pl.BlockSpec((each, rows_here, HEAD_DIM), lambda g: (g, 0, 0))] * heads_here,
        out_specs=pl.BlockSpec((rows_here, each * heads_here * HEAD_DIM), lambda g: (0, g)),
        out_shape=jax.ShapeDtypeStruct((rows_here, others * heads_here * HEAD_DIM), jnp.bfloat16),
        name="unpack",
    )(*returned)


def shards(q_fresh, k_fresh, v_fresh, k_stale, v_stale, rank, ends):
    heads_here = k_stale.shape[1] // HEAD_DIM
    others = q_fresh.shape[1] // k_stale.shape[1]
    rows_here = q_fresh.shape[0]
    arrived = []
    for head in range(heads_here):
        packed = pack((q_fresh, k_fresh, v_fresh), others, heads_here, head)
        arrived.append(lax.all_to_all(packed, "seq", split_axis=0, concat_axis=0, tiled=True))
    returned = []
    for head in range(heads_here):
        result = attend(arrived[head], k_stale, v_stale, rank, ends, head)
        result = result.reshape(others, rows_here, HEAD_DIM)
        returned.append(lax.all_to_all(result, "seq", split_axis=0, concat_axis=0, tiled=True))
    return unpack(returned)


def solution(mesh):
    return jax.shard_map(
        shards,
        mesh=mesh,
        in_specs=(
            P(("groups", "seq"), None),
            P(("groups", "seq"), None),
            P(("groups", "seq"), None),
            P("groups", "seq"),
            P("groups", "seq"),
            P("groups"),
            P("groups"),
        ),
        out_specs=P(("groups", "seq"), None),
        check_vma=False,
    )
```

```python
import functools
import math

import jax
import jax.numpy as jnp
from jax import lax
from jax.experimental import pallas as pl
from jax.experimental.pallas import tpu as pltpu
from jax.sharding import PartitionSpec as P


HEAD_DIM = 128
PATCH = 512


def attend_patch(p, rank_ref, ends_ref, query, k_ref, v_ref, ks_ref, vs_ref, out_ref, scratch):
    even, odd, top, total, mixed = scratch
    factor = math.log2(math.e) / math.sqrt(HEAD_DIM)
    mine = rank_ref[p]
    count = ends_ref[p] // PATCH
    top[...] = jnp.full(top.shape, -jnp.inf, jnp.float32)
    total[...] = jnp.zeros(total.shape, jnp.float32)
    mixed[...] = jnp.zeros(mixed.shape, jnp.float32)

    def chosen(j, new_ref, old_ref):
        at = pl.ds(pl.multiple_of(j * PATCH, PATCH), PATCH)
        return jnp.where(rank_ref[j] <= mine, new_ref[at, :], old_ref[at, :])

    def score(j):
        keys = chosen(jnp.minimum(j, count - 1), k_ref, ks_ref)
        return lax.dot_general(query, keys, (((1,), (1,)), ((), ())), preferred_element_type=jnp.float32)

    def fold(scores, j):
        before = top[...]
        higher = jnp.maximum(before, jnp.max(scores[...], axis=1, keepdims=True) * factor)
        top[...] = higher
        shrink = jnp.exp2(before - higher)
        sums = total[...] * shrink
        rounded = []
        for c in range(0, PATCH, HEAD_DIM):
            weight = jnp.exp2(scores[:, c:c + HEAD_DIM] * factor - higher)
            sums = sums + weight
            rounded.append(weight.astype(jnp.bfloat16))
        total[...] = sums
        weights = jnp.concatenate(rounded, axis=1)
        mixed[...] = mixed[...] * shrink + jnp.dot(
            weights, chosen(j, v_ref, vs_ref), preferred_element_type=jnp.float32
        )

    even[...] = score(0)

    def two(t, _):
        odd[...] = score(2 * t + 1)
        fold(even, 2 * t)

        @pl.when(2 * t + 1 < count)
        def _():
            even[...] = score(2 * t + 2)
            fold(odd, 2 * t + 1)

        return 0

    lax.fori_loop(0, (count + 1) // 2, two, 0)
    out_ref[...] = (mixed[...] / jnp.sum(total[...], axis=1, keepdims=True)).astype(jnp.bfloat16)


ATTEND_SCRATCH = [pltpu.VMEM((PATCH, PATCH), jnp.float32)] * 2 + [pltpu.VMEM((PATCH, HEAD_DIM), jnp.float32)] * 3


def attend_whole_kernel(rank_ref, ends_ref, q_ref, kf_ref, vf_ref, ks_ref, vs_ref, out_ref, *scratch):
    p = pl.program_id(0)
    flat = (q_ref.shape[0] * q_ref.shape[1], HEAD_DIM)
    query = q_ref.reshape(*flat)[pl.ds(pl.multiple_of(p * PATCH, PATCH), PATCH), :]
    keys, values = kf_ref.reshape(*flat), vf_ref.reshape(*flat)
    attend_patch(p, rank_ref, ends_ref, query, keys, values, ks_ref, vs_ref, out_ref, scratch)


def attend_whole(packed, k_stale, v_stale, rank, ends, head):
    shards_here, _, rows_here, _ = packed.shape
    total_rows = shards_here * rows_here
    part = [
        pl.BlockSpec((shards_here, None, rows_here, HEAD_DIM), lambda p, r, e, i=i: (0, i, 0, 0))
        for i in range(3)
    ]
    stale = pl.BlockSpec((total_rows, HEAD_DIM), lambda p, r, e: (0, head))
    return pl.pallas_call(
        attend_whole_kernel,
        grid_spec=pltpu.PrefetchScalarGridSpec(
            num_scalar_prefetch=2,
            grid=(rank.shape[0],),
            in_specs=[*part, stale, stale],
            out_specs=pl.BlockSpec((PATCH, HEAD_DIM), lambda p, r, e: (p, 0)),
            scratch_shapes=ATTEND_SCRATCH,
        ),
        out_shape=jax.ShapeDtypeStruct((total_rows, HEAD_DIM), jnp.bfloat16),
        name="attend_whole",
    )(rank, ends, packed, packed, packed, k_stale, v_stale)


def attend_parts_kernel(rank_ref, ends_ref, me_ref, *refs, peers):
    blocks = refs[:peers]
    ks_ref, vs_ref, out_ref, q_all, k_all, v_all, *scratch = refs[peers:]
    p = pl.program_id(0)
    rows_here = blocks[0].shape[1]

    @pl.when(p == 0)
    def _():
        for k in range(peers):
            at = pl.ds(pl.multiple_of((me_ref[0] ^ k) * rows_here, rows_here), rows_here)
            for i, ref in enumerate((q_all, k_all, v_all)):
                ref[at, :] = blocks[k][i]

    query = q_all[pl.ds(pl.multiple_of(p * PATCH, PATCH), PATCH), :]
    attend_patch(p, rank_ref, ends_ref, query, k_all, v_all, ks_ref, vs_ref, out_ref, scratch)


def attend_parts(blocks, k_stale, v_stale, rank, ends, me, head):
    peers = len(blocks)
    _, rows_here, _ = blocks[0].shape
    total_rows = peers * rows_here
    stale = pl.BlockSpec((total_rows, HEAD_DIM), lambda p, r, e, m: (0, head))
    return pl.pallas_call(
        functools.partial(attend_parts_kernel, peers=peers),
        grid_spec=pltpu.PrefetchScalarGridSpec(
            num_scalar_prefetch=3,
            grid=(rank.shape[0],),
            in_specs=[pl.BlockSpec(blocks[0].shape, lambda p, r, e, m: (0, 0, 0))] * peers + [stale, stale],
            out_specs=pl.BlockSpec((PATCH, HEAD_DIM), lambda p, r, e, m: (p, 0)),
            scratch_shapes=[pltpu.VMEM((total_rows, HEAD_DIM), jnp.bfloat16)] * 3 + ATTEND_SCRATCH,
        ),
        out_shape=jax.ShapeDtypeStruct((total_rows, HEAD_DIM), jnp.bfloat16),
        name="attend_parts",
    )(rank, ends, me, *blocks, k_stale, v_stale)


def pack_kernel(q_ref, k_ref, v_ref, out_ref, *, head, heads_here):
    for t in range(out_ref.shape[0]):
        at = (t * heads_here + head) * HEAD_DIM
        for i, ref in enumerate((q_ref, k_ref, v_ref)):
            out_ref[t, i] = ref[:, at:at + HEAD_DIM]


def pack(arrays, others, heads_here, head):
    rows_here = arrays[0].shape[0]
    each = math.gcd(others, 4)
    wide = each * heads_here * HEAD_DIM
    return pl.pallas_call(
        functools.partial(pack_kernel, head=head, heads_here=heads_here),
        grid=(others // each,),
        in_specs=[pl.BlockSpec((rows_here, wide), lambda g: (0, g))] * 3,
        out_specs=pl.BlockSpec((each, 3, rows_here, HEAD_DIM), lambda g: (g, 0, 0, 0)),
        out_shape=jax.ShapeDtypeStruct((others, 3, rows_here, HEAD_DIM), jnp.bfloat16),
        name="pack",
    )(*arrays)


def split_kernel(me_ref, q_ref, k_ref, v_ref, *outs, head, heads_here):
    for k, out_ref in enumerate(outs):
        at = pl.ds(pl.multiple_of(((me_ref[0] ^ k) * heads_here + head) * HEAD_DIM, HEAD_DIM), HEAD_DIM)
        for i, ref in enumerate((q_ref, k_ref, v_ref)):
            out_ref[i] = ref[:, at]


def split(arrays, me, peers, heads_here, head):
    rows_here = arrays[0].shape[0]
    shape = (3, rows_here, HEAD_DIM)
    return pl.pallas_call(
        functools.partial(split_kernel, head=head, heads_here=heads_here),
        grid_spec=pltpu.PrefetchScalarGridSpec(
            num_scalar_prefetch=1,
            grid=(1,),
            in_specs=[pl.BlockSpec(arrays[0].shape, lambda g, m: (0, 0))] * 3,
            out_specs=[pl.BlockSpec(shape, lambda g, m: (0, 0, 0))] * peers,
        ),
        out_shape=[jax.ShapeDtypeStruct(shape, jnp.bfloat16)] * peers,
        name="split",
    )(me, *arrays)


def unpack_kernel(*refs):
    out_ref = refs[-1]
    heads_here = len(refs) - 1
    for head in range(heads_here):
        for t in range(refs[head].shape[0]):
            at = (t * heads_here + head) * HEAD_DIM
            out_ref[:, at:at + HEAD_DIM] = refs[head][t]


def unpack(returned):
    heads_here = len(returned)
    others, rows_here, _ = returned[0].shape
    each = math.gcd(others, 4)
    return pl.pallas_call(
        unpack_kernel,
        grid=(others // each,),
        in_specs=[pl.BlockSpec((each, rows_here, HEAD_DIM), lambda g: (g, 0, 0))] * heads_here,
        out_specs=pl.BlockSpec((rows_here, each * heads_here * HEAD_DIM), lambda g: (0, g)),
        out_shape=jax.ShapeDtypeStruct((rows_here, others * heads_here * HEAD_DIM), jnp.bfloat16),
        name="unpack",
    )(*returned)


def shards(q_fresh, k_fresh, v_fresh, k_stale, v_stale, rank, ends):
    heads_here = k_stale.shape[1] // HEAD_DIM
    peers = q_fresh.shape[1] // k_stale.shape[1]
    rows_here = q_fresh.shape[0]
    fresh = (q_fresh, k_fresh, v_fresh)
    me = lax.axis_index("seq").astype(jnp.int32).reshape(1)

    def swap(array):
        return lax.all_to_all(array, "seq", split_axis=0, concat_axis=0, tiled=True)

    first = swap(pack(fresh, peers, heads_here, 0))
    later = []
    for head in range(1, heads_here):
        blocks = list(split(fresh, me, peers, heads_here, head))
        for k in (*range(1, peers // 2), *range(peers - 1, peers // 2 - 1, -1)):
            blocks[k] = lax.ppermute(blocks[k], "seq", [(s, s ^ k) for s in range(peers)])
        later.append(blocks)
    returned = []
    for head in range(heads_here):
        if head == 0:
            result = attend_whole(first, k_stale, v_stale, rank, ends, head)
        else:
            result = attend_parts(later[head - 1], k_stale, v_stale, rank, ends, me, head)
        returned.append(swap(result.reshape(peers, rows_here, HEAD_DIM)))
    return unpack(returned)


def solution(mesh):
    return jax.shard_map(
        shards,
        mesh=mesh,
        in_specs=(
            P(("groups", "seq"), None),
            P(("groups", "seq"), None),
            P(("groups", "seq"), None),
            P("groups", "seq"),
            P("groups", "seq"),
            P("groups"),
            P("groups"),
        ),
        out_specs=P(("groups", "seq"), None),
        check_vma=False,
    )
```

```python
import functools
import math

import jax
import jax.numpy as jnp
from jax import lax
from jax.experimental import pallas as pl
from jax.experimental.pallas import tpu as pltpu
from jax.sharding import PartitionSpec as P


HEAD_DIM = 128
PATCH = 512


def attend_patch(p, rank_ref, ends_ref, query, k_ref, v_ref, ks_ref, vs_ref, out_ref, scratch):
    even, odd, top, total, mixed = scratch
    factor = math.log2(math.e) / math.sqrt(HEAD_DIM)
    mine = rank_ref[p]
    count = ends_ref[p] // PATCH
    top[...] = jnp.full(top.shape, -jnp.inf, jnp.float32)
    total[...] = jnp.zeros(total.shape, jnp.float32)
    mixed[...] = jnp.zeros(mixed.shape, jnp.float32)

    def chosen(j, new_ref, old_ref):
        at = pl.ds(pl.multiple_of(j * PATCH, PATCH), PATCH)
        return jnp.where(rank_ref[j] <= mine, new_ref[at, :], old_ref[at, :])

    def score(j):
        keys = chosen(jnp.minimum(j, count - 1), k_ref, ks_ref)
        return lax.dot_general(query, keys, (((1,), (1,)), ((), ())), preferred_element_type=jnp.float32)

    def fold(scores, j):
        before = top[...]
        higher = jnp.maximum(before, jnp.max(scores[...], axis=1, keepdims=True) * factor)
        top[...] = higher
        shrink = jnp.exp2(before - higher)
        sums = total[...] * shrink
        rounded = []
        for c in range(0, PATCH, HEAD_DIM):
            weight = jnp.exp2(scores[:, c:c + HEAD_DIM] * factor - higher)
            sums = sums + weight
            rounded.append(weight.astype(jnp.bfloat16))
        total[...] = sums
        weights = jnp.concatenate(rounded, axis=1)
        mixed[...] = mixed[...] * shrink + jnp.dot(
            weights, chosen(j, v_ref, vs_ref), preferred_element_type=jnp.float32
        )

    even[...] = score(0)

    def two(t, _):
        odd[...] = score(2 * t + 1)
        fold(even, 2 * t)

        @pl.when(2 * t + 1 < count)
        def _():
            even[...] = score(2 * t + 2)
            fold(odd, 2 * t + 1)

        return 0

    lax.fori_loop(0, (count + 1) // 2, two, 0)
    out_ref[...] = (mixed[...] / jnp.sum(total[...], axis=1, keepdims=True)).astype(jnp.bfloat16)


ATTEND_SCRATCH = [pltpu.VMEM((PATCH, PATCH), jnp.float32)] * 2 + [pltpu.VMEM((PATCH, HEAD_DIM), jnp.float32)] * 3


def attend_whole_kernel(rank_ref, ends_ref, q_ref, kf_ref, vf_ref, ks_ref, vs_ref, out_ref, *scratch):
    p = pl.program_id(0)
    flat = (q_ref.shape[0] * q_ref.shape[1], HEAD_DIM)
    query = q_ref.reshape(*flat)[pl.ds(pl.multiple_of(p * PATCH, PATCH), PATCH), :]
    keys, values = kf_ref.reshape(*flat), vf_ref.reshape(*flat)
    attend_patch(p, rank_ref, ends_ref, query, keys, values, ks_ref, vs_ref, out_ref, scratch)


def attend_whole(packed, k_stale, v_stale, rank, ends, head):
    shards_here, _, rows_here, _ = packed.shape
    total_rows = shards_here * rows_here
    part = [
        pl.BlockSpec((shards_here, None, rows_here, HEAD_DIM), lambda p, r, e, i=i: (0, i, 0, 0))
        for i in range(3)
    ]
    stale = pl.BlockSpec((total_rows, HEAD_DIM), lambda p, r, e: (0, head))
    return pl.pallas_call(
        attend_whole_kernel,
        grid_spec=pltpu.PrefetchScalarGridSpec(
            num_scalar_prefetch=2,
            grid=(rank.shape[0],),
            in_specs=[*part, stale, stale],
            out_specs=pl.BlockSpec((PATCH, HEAD_DIM), lambda p, r, e: (p, 0)),
            scratch_shapes=ATTEND_SCRATCH,
        ),
        out_shape=jax.ShapeDtypeStruct((total_rows, HEAD_DIM), jnp.bfloat16),
        name="attend_whole",
    )(rank, ends, packed, packed, packed, k_stale, v_stale)


def attend_parts_kernel(rank_ref, ends_ref, me_ref, *refs, peers):
    blocks = refs[:peers]
    ks_ref, vs_ref, out_ref, q_all, k_all, v_all, *scratch = refs[peers:]
    p = pl.program_id(0)
    rows_here = blocks[0].shape[1]

    @pl.when(p == 0)
    def _():
        for k in range(peers):
            at = pl.ds(pl.multiple_of((me_ref[0] ^ k) * rows_here, rows_here), rows_here)
            for i, ref in enumerate((q_all, k_all, v_all)):
                ref[at, :] = blocks[k][i]

    query = q_all[pl.ds(pl.multiple_of(p * PATCH, PATCH), PATCH), :]
    attend_patch(p, rank_ref, ends_ref, query, k_all, v_all, ks_ref, vs_ref, out_ref, scratch)


def attend_parts(blocks, k_stale, v_stale, rank, ends, me, head):
    peers = len(blocks)
    _, rows_here, _ = blocks[0].shape
    total_rows = peers * rows_here
    stale = pl.BlockSpec((total_rows, HEAD_DIM), lambda p, r, e, m: (0, head))
    return pl.pallas_call(
        functools.partial(attend_parts_kernel, peers=peers),
        grid_spec=pltpu.PrefetchScalarGridSpec(
            num_scalar_prefetch=3,
            grid=(rank.shape[0],),
            in_specs=[pl.BlockSpec(blocks[0].shape, lambda p, r, e, m: (0, 0, 0))] * peers + [stale, stale],
            out_specs=pl.BlockSpec((PATCH, HEAD_DIM), lambda p, r, e, m: (p, 0)),
            scratch_shapes=[pltpu.VMEM((total_rows, HEAD_DIM), jnp.bfloat16)] * 3 + ATTEND_SCRATCH,
        ),
        out_shape=jax.ShapeDtypeStruct((total_rows, HEAD_DIM), jnp.bfloat16),
        name="attend_parts",
    )(rank, ends, me, *blocks, k_stale, v_stale)


def pack_kernel(q_ref, k_ref, v_ref, out_ref, held, read_sem, write_sem, *, head, heads_here):
    reads, writes = [], []
    for t in range(out_ref.shape[0]):
        at = (t * heads_here + head) * HEAD_DIM
        reads.append([
            pltpu.make_async_copy(ref.at[:, at:at + HEAD_DIM], held.at[t, i], read_sem.at[t, i])
            for i, ref in enumerate((q_ref, k_ref, v_ref))
        ])
        for copy in reads[t]:
            copy.start()
    for t in range(out_ref.shape[0]):
        for copy in reads[t]:
            copy.wait()
        writes.append(pltpu.make_async_copy(held.at[t], out_ref.at[t], write_sem.at[t]))
        writes[t].start()
    for copy in writes:
        copy.wait()


def pack(arrays, others, heads_here, head):
    rows_here = arrays[0].shape[0]
    shape = (others, 3, rows_here, HEAD_DIM)
    return pl.pallas_call(
        functools.partial(pack_kernel, head=head, heads_here=heads_here),
        in_specs=[pl.BlockSpec(memory_space=pl.ANY)] * 3,
        out_specs=pl.BlockSpec(memory_space=pl.ANY),
        out_shape=jax.ShapeDtypeStruct(shape, jnp.bfloat16),
        scratch_shapes=[
            pltpu.VMEM(shape, jnp.bfloat16),
            pltpu.SemaphoreType.DMA((others, 3)),
            pltpu.SemaphoreType.DMA((others,)),
        ],
        name="pack",
    )(*arrays)


def split_kernel(me_ref, q_ref, k_ref, v_ref, *outs, head, heads_here):
    for k, out_ref in enumerate(outs):
        at = pl.ds(pl.multiple_of(((me_ref[0] ^ k) * heads_here + head) * HEAD_DIM, HEAD_DIM), HEAD_DIM)
        for i, ref in enumerate((q_ref, k_ref, v_ref)):
            out_ref[i] = ref[:, at]


def split(arrays, me, peers, heads_here, head):
    rows_here = arrays[0].shape[0]
    shape = (3, rows_here, HEAD_DIM)
    return pl.pallas_call(
        functools.partial(split_kernel, head=head, heads_here=heads_here),
        grid_spec=pltpu.PrefetchScalarGridSpec(
            num_scalar_prefetch=1,
            grid=(1,),
            in_specs=[pl.BlockSpec(arrays[0].shape, lambda g, m: (0, 0))] * 3,
            out_specs=[pl.BlockSpec(shape, lambda g, m: (0, 0, 0))] * peers,
        ),
        out_shape=[jax.ShapeDtypeStruct(shape, jnp.bfloat16)] * peers,
        name="split",
    )(me, *arrays)


def unpack_kernel(*refs):
    out_ref = refs[-1]
    heads_here = len(refs) - 1
    for head in range(heads_here):
        for t in range(refs[head].shape[0]):
            at = (t * heads_here + head) * HEAD_DIM
            out_ref[:, at:at + HEAD_DIM] = refs[head][t]


def unpack(returned):
    heads_here = len(returned)
    others, rows_here, _ = returned[0].shape
    each = math.gcd(others, 8)
    return pl.pallas_call(
        unpack_kernel,
        grid=(others // each,),
        in_specs=[pl.BlockSpec((each, rows_here, HEAD_DIM), lambda g: (g, 0, 0))] * heads_here,
        out_specs=pl.BlockSpec((rows_here, each * heads_here * HEAD_DIM), lambda g: (0, g)),
        out_shape=jax.ShapeDtypeStruct((rows_here, others * heads_here * HEAD_DIM), jnp.bfloat16),
        name="unpack",
    )(*returned)


def shards(q_fresh, k_fresh, v_fresh, k_stale, v_stale, rank, ends):
    heads_here = k_stale.shape[1] // HEAD_DIM
    peers = q_fresh.shape[1] // k_stale.shape[1]
    rows_here = q_fresh.shape[0]
    fresh = (q_fresh, k_fresh, v_fresh)
    me = lax.axis_index("seq").astype(jnp.int32).reshape(1)

    def swap(array):
        return lax.all_to_all(array, "seq", split_axis=0, concat_axis=0, tiled=True)

    first = swap(pack(fresh, peers, heads_here, 0))
    later = []
    for head in range(1, heads_here):
        blocks = list(split(fresh, me, peers, heads_here, head))
        for k in range(1, peers):
            blocks[k] = lax.ppermute(blocks[k], "seq", [(s, s ^ k) for s in range(peers)])
        later.append(blocks)
    returned = []
    for head in range(heads_here):
        if head == 0:
            result = attend_whole(first, k_stale, v_stale, rank, ends, head)
        else:
            result = attend_parts(later[head - 1], k_stale, v_stale, rank, ends, me, head)
        returned.append(swap(result.reshape(peers, rows_here, HEAD_DIM)))
    return unpack(returned)


def solution(mesh):
    return jax.shard_map(
        shards,
        mesh=mesh,
        in_specs=(
            P(("groups", "seq"), None),
            P(("groups", "seq"), None),
            P(("groups", "seq"), None),
            P("groups", "seq"),
            P("groups", "seq"),
            P("groups"),
            P("groups"),
        ),
        out_specs=P(("groups", "seq"), None),
        check_vma=False,
    )
```

```python
import functools
import math

import jax
import jax.numpy as jnp
from jax import lax
from jax.experimental import pallas as pl
from jax.experimental.pallas import tpu as pltpu
from jax.sharding import PartitionSpec as P


HEAD_DIM = 128
PATCH = 512


def attend_all(rank_ref, ends_ref, q_ref, k_ref, v_ref, ks_ref, vs_ref, out_ref, scratch):
    even, odd, top, total, mixed = scratch
    factor = math.log2(math.e) / math.sqrt(HEAD_DIM)
    patches = rank_ref.shape[0]

    def rows_of(patch):
        return pl.ds(pl.multiple_of(patch * PATCH, PATCH), PATCH)

    def blocks_of(p):
        return ends_ref[p] // PATCH

    def chosen(p, j, new_ref, old_ref):
        return jnp.where(rank_ref[j] <= rank_ref[p], new_ref[rows_of(j), :], old_ref[rows_of(j), :])

    def after(p, j):
        last = j + 1 >= blocks_of(p)
        return jnp.where(last, jnp.minimum(p + 1, patches - 1), p), jnp.where(last, 0, j + 1)

    def score(scores, p, j):
        scores[...] = lax.dot_general(
            q_ref[rows_of(p), :],
            chosen(p, j, k_ref, ks_ref),
            (((1,), (1,)), ((), ())),
            preferred_element_type=jnp.float32,
        )

    def clear():
        top[...] = jnp.full(top.shape, -jnp.inf, jnp.float32)
        total[...] = jnp.zeros(total.shape, jnp.float32)
        mixed[...] = jnp.zeros(mixed.shape, jnp.float32)

    def fold(scores, p, j):
        before = top[...]
        higher = jnp.maximum(before, jnp.max(scores[...], axis=1, keepdims=True) * factor)
        top[...] = higher
        shrink = jnp.exp2(before - higher)
        sums = total[...] * shrink
        rounded = []
        for c in range(0, PATCH, HEAD_DIM):
            weight = jnp.exp2(scores[:, c:c + HEAD_DIM] * factor - higher)
            sums = sums + weight
            rounded.append(weight.astype(jnp.bfloat16))
        total[...] = sums
        weights = jnp.concatenate(rounded, axis=1)
        mixed[...] = mixed[...] * shrink + jnp.dot(
            weights, chosen(p, j, v_ref, vs_ref), preferred_element_type=jnp.float32
        )

        @pl.when(j + 1 == blocks_of(p))
        def _():
            out_ref[rows_of(p), :] = (mixed[...] / jnp.sum(total[...], axis=1, keepdims=True)).astype(jnp.bfloat16)
            clear()

    pairs = blocks_of(0)
    for p in range(1, patches):
        pairs = pairs + blocks_of(p)
    clear()
    score(even, 0, 0)

    def two(t, at):
        then = after(*at)
        score(odd, *then)
        fold(even, *at)
        beyond = after(*then)

        @pl.when(2 * t + 1 < pairs)
        def _():
            score(even, *beyond)
            fold(odd, *then)

        return beyond

    lax.fori_loop(0, (pairs + 1) // 2, two, (jnp.int32(0), jnp.int32(0)))


ATTEND_SCRATCH = [pltpu.VMEM((PATCH, PATCH), jnp.float32)] * 2 + [pltpu.VMEM((PATCH, HEAD_DIM), jnp.float32)] * 3


def attend_whole_kernel(rank_ref, ends_ref, q_ref, kf_ref, vf_ref, ks_ref, vs_ref, out_ref, *scratch):
    flat = (q_ref.shape[0] * q_ref.shape[1], HEAD_DIM)
    fresh = [ref.reshape(*flat) for ref in (q_ref, kf_ref, vf_ref)]
    attend_all(rank_ref, ends_ref, *fresh, ks_ref, vs_ref, out_ref, scratch)


def attend_whole(packed, k_stale, v_stale, rank, ends, head):
    shards_here, _, rows_here, _ = packed.shape
    total_rows = shards_here * rows_here
    part = [
        pl.BlockSpec((shards_here, None, rows_here, HEAD_DIM), lambda p, r, e, i=i: (0, i, 0, 0))
        for i in range(3)
    ]
    stale = pl.BlockSpec((total_rows, HEAD_DIM), lambda p, r, e: (0, head))
    return pl.pallas_call(
        attend_whole_kernel,
        grid_spec=pltpu.PrefetchScalarGridSpec(
            num_scalar_prefetch=2,
            grid=(1,),
            in_specs=[*part, stale, stale],
            out_specs=pl.BlockSpec((total_rows, HEAD_DIM), lambda p, r, e: (0, 0)),
            scratch_shapes=ATTEND_SCRATCH,
        ),
        out_shape=jax.ShapeDtypeStruct((total_rows, HEAD_DIM), jnp.bfloat16),
        name="attend_whole",
    )(rank, ends, packed, packed, packed, k_stale, v_stale)


def attend_parts_kernel(rank_ref, ends_ref, me_ref, *refs, peers):
    blocks = refs[:peers]
    ks_ref, vs_ref, out_ref, *fresh = refs[peers:peers + 6]
    rows_here = blocks[0].shape[1]
    for k in range(peers):
        at = pl.ds(pl.multiple_of((me_ref[0] ^ k) * rows_here, rows_here), rows_here)
        for i, ref in enumerate(fresh):
            ref[at, :] = blocks[k][i]
    attend_all(rank_ref, ends_ref, *fresh, ks_ref, vs_ref, out_ref, refs[peers + 6:])


def attend_parts(blocks, k_stale, v_stale, rank, ends, me, head):
    peers = len(blocks)
    _, rows_here, _ = blocks[0].shape
    total_rows = peers * rows_here
    stale = pl.BlockSpec((total_rows, HEAD_DIM), lambda p, r, e, m: (0, head))
    return pl.pallas_call(
        functools.partial(attend_parts_kernel, peers=peers),
        grid_spec=pltpu.PrefetchScalarGridSpec(
            num_scalar_prefetch=3,
            grid=(1,),
            in_specs=[pl.BlockSpec(blocks[0].shape, lambda p, r, e, m: (0, 0, 0))] * peers + [stale, stale],
            out_specs=pl.BlockSpec((total_rows, HEAD_DIM), lambda p, r, e, m: (0, 0)),
            scratch_shapes=[pltpu.VMEM((total_rows, HEAD_DIM), jnp.bfloat16)] * 3 + ATTEND_SCRATCH,
        ),
        out_shape=jax.ShapeDtypeStruct((total_rows, HEAD_DIM), jnp.bfloat16),
        name="attend_parts",
    )(rank, ends, me, *blocks, k_stale, v_stale)


def pack_kernel(q_ref, k_ref, v_ref, out_ref, held, read_sem, write_sem, *, head, heads_here):
    reads, writes = [], []
    for t in range(out_ref.shape[0]):
        at = (t * heads_here + head) * HEAD_DIM
        reads.append([
            pltpu.make_async_copy(ref.at[:, at:at + HEAD_DIM], held.at[t, i], read_sem.at[t, i])
            for i, ref in enumerate((q_ref, k_ref, v_ref))
        ])
        for copy in reads[t]:
            copy.start()
    for t in range(out_ref.shape[0]):
        for copy in reads[t]:
            copy.wait()
        writes.append(pltpu.make_async_copy(held.at[t], out_ref.at[t], write_sem.at[t]))
        writes[t].start()
    for copy in writes:
        copy.wait()


def pack(arrays, others, heads_here, head):
    rows_here = arrays[0].shape[0]
    shape = (others, 3, rows_here, HEAD_DIM)
    return pl.pallas_call(
        functools.partial(pack_kernel, head=head, heads_here=heads_here),
        in_specs=[pl.BlockSpec(memory_space=pl.ANY)] * 3,
        out_specs=pl.BlockSpec(memory_space=pl.ANY),
        out_shape=jax.ShapeDtypeStruct(shape, jnp.bfloat16),
        scratch_shapes=[
            pltpu.VMEM(shape, jnp.bfloat16),
            pltpu.SemaphoreType.DMA((others, 3)),
            pltpu.SemaphoreType.DMA((others,)),
        ],
        name="pack",
    )(*arrays)


def split_kernel(me_ref, q_ref, k_ref, v_ref, *outs, head, heads_here):
    for k, out_ref in enumerate(outs):
        at = pl.ds(pl.multiple_of(((me_ref[0] ^ k) * heads_here + head) * HEAD_DIM, HEAD_DIM), HEAD_DIM)
        for i, ref in enumerate((q_ref, k_ref, v_ref)):
            out_ref[i] = ref[:, at]


def split(arrays, me, peers, heads_here, head):
    rows_here = arrays[0].shape[0]
    shape = (3, rows_here, HEAD_DIM)
    return pl.pallas_call(
        functools.partial(split_kernel, head=head, heads_here=heads_here),
        grid_spec=pltpu.PrefetchScalarGridSpec(
            num_scalar_prefetch=1,
            grid=(1,),
            in_specs=[pl.BlockSpec(arrays[0].shape, lambda g, m: (0, 0))] * 3,
            out_specs=[pl.BlockSpec(shape, lambda g, m: (0, 0, 0))] * peers,
        ),
        out_shape=[jax.ShapeDtypeStruct(shape, jnp.bfloat16)] * peers,
        name="split",
    )(me, *arrays)


def unpack_kernel(*refs):
    out_ref = refs[-1]
    heads_here = len(refs) - 1
    for head in range(heads_here):
        for t in range(refs[head].shape[0]):
            at = (t * heads_here + head) * HEAD_DIM
            out_ref[:, at:at + HEAD_DIM] = refs[head][t]


def unpack(returned):
    heads_here = len(returned)
    others, rows_here, _ = returned[0].shape
    each = math.gcd(others, 8)
    return pl.pallas_call(
        unpack_kernel,
        grid=(others // each,),
        in_specs=[pl.BlockSpec((each, rows_here, HEAD_DIM), lambda g: (g, 0, 0))] * heads_here,
        out_specs=pl.BlockSpec((rows_here, each * heads_here * HEAD_DIM), lambda g: (0, g)),
        out_shape=jax.ShapeDtypeStruct((rows_here, others * heads_here * HEAD_DIM), jnp.bfloat16),
        name="unpack",
    )(*returned)


def shards(q_fresh, k_fresh, v_fresh, k_stale, v_stale, rank, ends):
    heads_here = k_stale.shape[1] // HEAD_DIM
    peers = q_fresh.shape[1] // k_stale.shape[1]
    rows_here = q_fresh.shape[0]
    fresh = (q_fresh, k_fresh, v_fresh)
    me = lax.axis_index("seq").astype(jnp.int32).reshape(1)

    def swap(array):
        return lax.all_to_all(array, "seq", split_axis=0, concat_axis=0, tiled=True)

    first = swap(pack(fresh, peers, heads_here, 0))
    later = []
    for head in range(1, heads_here):
        blocks = list(split(fresh, me, peers, heads_here, head))
        for k in range(1, peers):
            blocks[k] = lax.ppermute(blocks[k], "seq", [(s, s ^ k) for s in range(peers)])
        later.append(blocks)
    returned = []
    for head in range(heads_here):
        if head == 0:
            result = attend_whole(first, k_stale, v_stale, rank, ends, head)
        else:
            result = attend_parts(later[head - 1], k_stale, v_stale, rank, ends, me, head)
        returned.append(swap(result.reshape(peers, rows_here, HEAD_DIM)))
    return unpack(returned)


def solution(mesh):
    return jax.shard_map(
        shards,
        mesh=mesh,
        in_specs=(
            P(("groups", "seq"), None),
            P(("groups", "seq"), None),
            P(("groups", "seq"), None),
            P("groups", "seq"),
            P("groups", "seq"),
            P("groups"),
            P("groups"),
        ),
        out_specs=P(("groups", "seq"), None),
        check_vma=False,
    )
```

```python
import functools
import math

import jax
import jax.numpy as jnp
from jax import lax
from jax.experimental import pallas as pl
from jax.experimental.pallas import tpu as pltpu
from jax.sharding import PartitionSpec as P


HEAD_DIM = 128
PATCH = 512


def attend_all(rank_ref, ends_ref, q_ref, k_ref, v_ref, ks_ref, vs_ref, out_ref, scratch):
    even, odd, top, total, mixed = scratch
    factor = math.log2(math.e) / math.sqrt(HEAD_DIM)
    patches = rank_ref.shape[0]

    def rows_of(patch):
        return pl.ds(pl.multiple_of(patch * PATCH, PATCH), PATCH)

    def blocks_of(p):
        return ends_ref[p] // PATCH

    def chosen(p, j, new_ref, old_ref):
        return jnp.where(rank_ref[j] <= rank_ref[p], new_ref[rows_of(j), :], old_ref[rows_of(j), :])

    def after(p, j):
        last = j + 1 >= blocks_of(p)
        return jnp.where(last, jnp.minimum(p + 1, patches - 1), p), jnp.where(last, 0, j + 1)

    def score(scores, p, j):
        scores[...] = lax.dot_general(
            q_ref[rows_of(p), :],
            chosen(p, j, k_ref, ks_ref),
            (((1,), (1,)), ((), ())),
            preferred_element_type=jnp.float32,
        )

    def clear():
        top[...] = jnp.full(top.shape, -jnp.inf, jnp.float32)
        total[...] = jnp.zeros(total.shape, jnp.float32)
        mixed[...] = jnp.zeros(mixed.shape, jnp.float32)

    def fold(scores, p, j):
        before = top[...]
        higher = jnp.maximum(before, jnp.max(scores[...], axis=1, keepdims=True) * factor)
        top[...] = higher
        shrink = jnp.exp2(before - higher)
        sums = total[...] * shrink
        rounded = []
        for c in range(0, PATCH, HEAD_DIM):
            weight = jnp.exp2(scores[:, c:c + HEAD_DIM] * factor - higher)
            sums = sums + weight
            rounded.append(weight.astype(jnp.bfloat16))
        total[...] = sums
        weights = jnp.concatenate(rounded, axis=1)
        mixed[...] = mixed[...] * shrink + jnp.dot(
            weights, chosen(p, j, v_ref, vs_ref), preferred_element_type=jnp.float32
        )

        @pl.when(j + 1 == blocks_of(p))
        def _():
            out_ref[rows_of(p), :] = (mixed[...] / jnp.sum(total[...], axis=1, keepdims=True)).astype(jnp.bfloat16)
            clear()

    pairs = blocks_of(0)
    for p in range(1, patches):
        pairs = pairs + blocks_of(p)
    clear()
    score(even, 0, 0)

    def two(t, at):
        then = after(*at)
        score(odd, *then)
        fold(even, *at)
        beyond = after(*then)

        @pl.when(2 * t + 1 < pairs)
        def _():
            score(even, *beyond)
            fold(odd, *then)

        return beyond

    lax.fori_loop(0, (pairs + 1) // 2, two, (jnp.int32(0), jnp.int32(0)))


ATTEND_SCRATCH = [pltpu.VMEM((PATCH, PATCH), jnp.float32)] * 2 + [pltpu.VMEM((PATCH, HEAD_DIM), jnp.float32)] * 3


def attend_whole_kernel(rank_ref, ends_ref, packed_ref, ks_ref, vs_ref, out_ref, *refs):
    fresh, scratch = refs[:3], refs[3:]
    peers, _, rows_here, _ = packed_ref.shape
    for t in range(peers):
        for i, ref in enumerate(fresh):
            ref[t * rows_here:(t + 1) * rows_here, :] = packed_ref[t, i]
    attend_all(rank_ref, ends_ref, *fresh, ks_ref, vs_ref, out_ref, scratch)


def attend_whole(packed, k_stale, v_stale, rank, ends, head):
    peers, _, rows_here, _ = packed.shape
    total_rows = peers * rows_here
    stale = pl.BlockSpec((total_rows, HEAD_DIM), lambda p, r, e: (0, head))
    return pl.pallas_call(
        attend_whole_kernel,
        grid_spec=pltpu.PrefetchScalarGridSpec(
            num_scalar_prefetch=2,
            grid=(1,),
            in_specs=[pl.BlockSpec(memory_space=pltpu.VMEM), stale, stale],
            out_specs=pl.BlockSpec((total_rows, HEAD_DIM), lambda p, r, e: (0, 0)),
            scratch_shapes=[pltpu.VMEM((total_rows, HEAD_DIM), jnp.bfloat16)] * 3 + ATTEND_SCRATCH,
        ),
        out_shape=jax.ShapeDtypeStruct((total_rows, HEAD_DIM), jnp.bfloat16),
        compiler_params=pltpu.CompilerParams(vmem_limit_bytes=61 << 20),
        name="attend_whole",
    )(rank, ends, packed, k_stale, v_stale)


def attend_parts_kernel(rank_ref, ends_ref, me_ref, *refs, peers):
    blocks = refs[:peers]
    ks_ref, vs_ref, out_ref, *fresh = refs[peers:peers + 6]
    rows_here = blocks[0].shape[1]
    for k in range(peers):
        at = pl.ds(pl.multiple_of((me_ref[0] ^ k) * rows_here, rows_here), rows_here)
        for i, ref in enumerate(fresh):
            ref[at, :] = blocks[k][i]
    attend_all(rank_ref, ends_ref, *fresh, ks_ref, vs_ref, out_ref, refs[peers + 6:])


def attend_parts(blocks, k_stale, v_stale, rank, ends, me, head):
    peers = len(blocks)
    _, rows_here, _ = blocks[0].shape
    total_rows = peers * rows_here
    stale = pl.BlockSpec((total_rows, HEAD_DIM), lambda p, r, e, m: (0, head))
    return pl.pallas_call(
        functools.partial(attend_parts_kernel, peers=peers),
        grid_spec=pltpu.PrefetchScalarGridSpec(
            num_scalar_prefetch=3,
            grid=(1,),
            in_specs=[pl.BlockSpec(memory_space=pltpu.VMEM)] * peers + [stale, stale],
            out_specs=pl.BlockSpec((total_rows, HEAD_DIM), lambda p, r, e, m: (0, 0)),
            scratch_shapes=[pltpu.VMEM((total_rows, HEAD_DIM), jnp.bfloat16)] * 3 + ATTEND_SCRATCH,
        ),
        out_shape=jax.ShapeDtypeStruct((total_rows, HEAD_DIM), jnp.bfloat16),
        compiler_params=pltpu.CompilerParams(vmem_limit_bytes=24 << 20),
        name="attend_parts",
    )(rank, ends, me, *blocks, k_stale, v_stale)


def pack_kernel(q_ref, k_ref, v_ref, out_ref, held, read_sem, write_sem, *, head, heads_here):
    reads, writes = [], []
    for t in range(out_ref.shape[0]):
        at = (t * heads_here + head) * HEAD_DIM
        reads.append([
            pltpu.make_async_copy(ref.at[:, at:at + HEAD_DIM], held.at[t, i], read_sem.at[t, i])
            for i, ref in enumerate((q_ref, k_ref, v_ref))
        ])
        for copy in reads[t]:
            copy.start()
    for t in range(out_ref.shape[0]):
        for copy in reads[t]:
            copy.wait()
        writes.append(pltpu.make_async_copy(held.at[t], out_ref.at[t], write_sem.at[t]))
        writes[t].start()
    for copy in writes:
        copy.wait()


def pack(arrays, others, heads_here, head):
    rows_here = arrays[0].shape[0]
    shape = (others, 3, rows_here, HEAD_DIM)
    return pl.pallas_call(
        functools.partial(pack_kernel, head=head, heads_here=heads_here),
        in_specs=[pl.BlockSpec(memory_space=pl.ANY)] * 3,
        out_specs=pl.BlockSpec(memory_space=pl.ANY),
        out_shape=jax.ShapeDtypeStruct(shape, jnp.bfloat16),
        scratch_shapes=[
            pltpu.VMEM(shape, jnp.bfloat16),
            pltpu.SemaphoreType.DMA((others, 3)),
            pltpu.SemaphoreType.DMA((others,)),
        ],
        name="pack",
    )(*arrays)


def split_kernel(me_ref, q_ref, k_ref, v_ref, *outs, head, heads_here):
    for k, out_ref in enumerate(outs):
        at = pl.ds(pl.multiple_of(((me_ref[0] ^ k) * heads_here + head) * HEAD_DIM, HEAD_DIM), HEAD_DIM)
        for i, ref in enumerate((q_ref, k_ref, v_ref)):
            out_ref[i] = ref[:, at]


def split(arrays, me, peers, heads_here, head):
    rows_here = arrays[0].shape[0]
    shape = (3, rows_here, HEAD_DIM)
    return pl.pallas_call(
        functools.partial(split_kernel, head=head, heads_here=heads_here),
        grid_spec=pltpu.PrefetchScalarGridSpec(
            num_scalar_prefetch=1,
            grid=(1,),
            in_specs=[pl.BlockSpec(arrays[0].shape, lambda g, m: (0, 0))] * 3,
            out_specs=[pl.BlockSpec(shape, lambda g, m: (0, 0, 0))] * peers,
        ),
        out_shape=[jax.ShapeDtypeStruct(shape, jnp.bfloat16)] * peers,
        compiler_params=pltpu.CompilerParams(vmem_limit_bytes=24 << 20),
        name="split",
    )(me, *arrays)


def unpack_kernel(*refs):
    out_ref = refs[-1]
    heads_here = len(refs) - 1
    for head in range(heads_here):
        for t in range(refs[head].shape[0]):
            at = (t * heads_here + head) * HEAD_DIM
            out_ref[:, at:at + HEAD_DIM] = refs[head][t]


def unpack(returned):
    heads_here = len(returned)
    others, rows_here, _ = returned[0].shape
    each = math.gcd(others, 8)
    return pl.pallas_call(
        unpack_kernel,
        grid=(others // each,),
        in_specs=[pl.BlockSpec((each, rows_here, HEAD_DIM), lambda g: (g, 0, 0))] * heads_here,
        out_specs=pl.BlockSpec((rows_here, each * heads_here * HEAD_DIM), lambda g: (0, g)),
        out_shape=jax.ShapeDtypeStruct((rows_here, others * heads_here * HEAD_DIM), jnp.bfloat16),
        compiler_params=pltpu.CompilerParams(vmem_limit_bytes=24 << 20),
        name="unpack",
    )(*returned)


def shards(q_fresh, k_fresh, v_fresh, k_stale, v_stale, rank, ends):
    heads_here = k_stale.shape[1] // HEAD_DIM
    peers = q_fresh.shape[1] // k_stale.shape[1]
    rows_here = q_fresh.shape[0]
    fresh = (q_fresh, k_fresh, v_fresh)
    me = lax.axis_index("seq").astype(jnp.int32).reshape(1)

    def swap(array):
        return lax.all_to_all(array, "seq", split_axis=0, concat_axis=0, tiled=True)

    first = swap(pack(fresh, peers, heads_here, 0))
    later = []
    for head in range(1, heads_here):
        blocks = list(split(fresh, me, peers, heads_here, head))
        for k in range(1, peers):
            blocks[k] = lax.ppermute(blocks[k], "seq", [(s, s ^ k) for s in range(peers)])
        later.append(blocks)
    returned = []
    for head in range(heads_here):
        if head == 0:
            result = attend_whole(first, k_stale, v_stale, rank, ends, head)
        else:
            result = attend_parts(later[head - 1], k_stale, v_stale, rank, ends, me, head)
        returned.append(swap(result.reshape(peers, rows_here, HEAD_DIM)))
    return unpack(returned)


def solution(mesh):
    return jax.shard_map(
        shards,
        mesh=mesh,
        in_specs=(
            P(("groups", "seq"), None),
            P(("groups", "seq"), None),
            P(("groups", "seq"), None),
            P("groups", "seq"),
            P("groups", "seq"),
            P("groups"),
            P("groups"),
        ),
        out_specs=P(("groups", "seq"), None),
        check_vma=False,
    )
```
